512 devices in a mesh: dp: 8 (over y, core), ctx: 64 (over z, x).
Axes of the slice: x: 4, y: 4, z: 16, core: 2. Of those that a mesh axis runs over, the one named last changes fastest.
Arguments:
- queries: bfloat16 [8, 8192, 1024], P('dp', 'ctx'), may hold values from -6 to 6
- keys: bfloat16 [8, 8192, 1024], P('dp', 'ctx'), may hold values from -6 to 6
- values: bfloat16 [8, 8192, 1024], P('dp', 'ctx'), may hold values from -6 to 6
- log_decay: float32 [8, 8, 8192], P('dp', None, 'ctx'), may hold values from -2 to 0
- gain: float32 [1024], replicated, may hold values from 0.1 to 1.9
- out_grad: bfloat16 [8, 8192, 1024], P('dp', 'ctx'), may hold values from -16 to 16
Outputs:
- query_grad: bfloat16 [8, 8192, 1024], P('dp', 'ctx')
- key_grad: bfloat16 [8, 8192, 1024], P('dp', 'ctx')
- value_grad: bfloat16 [8, 8192, 1024], P('dp', 'ctx')
- gain_grad: float32 [1024], P('ctx')
The draws below stay inside these ranges and needn't reach their ends.
All inputs are finite; a program needn't handle non-finite values.
Results may differ from the reference program's by a relative error of at most 0.0059.
Values sent between devices are 32-bit elements; how exact they have to be, the bound alone decides.
A program may use at most 128 MiB of HBM per device.

```python
import math
import jax
import jax.numpy as jnp
from jax import lax

E = 128
WINDOW_HEADS = 8
TOK_DEV = 128
SUDDEN_DROPS = 3
SEQUENCE_LENGTH = 8192
BATCH_COUNT = 8


def draw_log_decay(key, part):
    split_points = jax.random.split(key, 7)
    heads_order = jax.random.permutation(split_points[0], WINDOW_HEADS)
    fast_count = WINDOW_HEADS // 2
    fast_heads = heads_order < fast_count
    fast_rate = jnp.exp(jax.random.uniform(split_points[1], (WINDOW_HEADS,), jnp.float32, math.log(1.0 / 50.0), math.log(1.0 / 30.0)))
    slow_rate = jnp.exp(jax.random.uniform(split_points[2], (WINDOW_HEADS,), jnp.float32, math.log(0.02), math.log(0.08))) / SEQUENCE_LENGTH
    baseline_decay_rate = jnp.where(fast_heads, fast_rate, slow_rate)
    block_multiplier = jnp.exp(jax.random.uniform(split_points[3], (BATCH_COUNT, WINDOW_HEADS, SEQUENCE_LENGTH // TOK_DEV), jnp.float32, math.log(0.5), math.log(1.5)))
    block_multiplier = jnp.repeat(block_multiplier, TOK_DEV, axis=2)
    decay_jitter = jnp.exp(jax.random.uniform(split_points[4], (BATCH_COUNT, WINDOW_HEADS, SEQUENCE_LENGTH), jnp.float32, -0.7, 0.7))
    sudden_drop_positions = jax.random.randint(split_points[5], (BATCH_COUNT, SUDDEN_DROPS), 0, SEQUENCE_LENGTH)
    sudden_drop_amounts = jax.random.uniform(split_points[6], (BATCH_COUNT, WINDOW_HEADS, SUDDEN_DROPS), jnp.float32, 0.22, 0.6)
    position_index = jnp.arange(SEQUENCE_LENGTH)
    sudden_drop_flags = (position_index[None, None, :] == sudden_drop_positions[:, :, None]).astype(jnp.float32)
    sudden_drops = jnp.sum(sudden_drop_amounts[:, :, :, None] * sudden_drop_flags[:, None, :, :], axis=2)
    return -(baseline_decay_rate[None, :, None] * block_multiplier * decay_jitter) - sudden_drops


def spiked(values, own_key, source, target, blocks, factor):
    def block_of(position):
        return (jnp.arange(values.shape[position]) // (values.shape[position] // blocks)).reshape((-1,) + (1,) * (values.ndim - 1 - position))

    one_side = jax.random.permutation(own_key, blocks)[block_of(target)]
    second = (block_of(target) + blocks // 2) % blocks
    return jnp.where((block_of(source) == one_side) | (block_of(source) == second), factor * values, values)


def shard_levels(rng, dims, shards, smallest, largest):
    factor_of, own = 1.0, jax.random.fold_in(rng, 6)
    for axis_at, blocks in shards:
        draws = jnp.exp(jax.random.uniform(jax.random.fold_in(own, axis_at), (blocks,), jnp.float32, smallest / len(shards), largest / len(shards)))
        factor_of = factor_of * jnp.repeat(draws, dims[axis_at] // blocks).reshape([-1 if axis == axis_at else 1 for axis in range(len(dims))])
    return factor_of


def normal_values(stream_key, dims, deviation, reach, cuts=(), held_as=jnp.bfloat16):
    result = deviation * jax.random.normal(stream_key, dims, jnp.float32)
    if cuts:
        result = result * shard_levels(stream_key, dims, cuts, -0.22, 0.18)
    return jnp.clip(result, -reach, reach).astype(held_as)


def bell_draw_with(key, dims, width, limit, pieces, heavy, kind=jnp.bfloat16):
    values = width * jax.random.normal(key, dims, jnp.float32)
    if pieces:
        values = values * shard_levels(key, dims, pieces, -0.22, 0.18)
    return jnp.clip(spiked(values, jax.random.fold_in(key, 3), *heavy), -limit, limit).astype(kind)


def setup_inputs(seed: int = 0) -> dict:
    streams_of = jax.random.split(jax.random.key(seed), 7)
    queries = normal_values(streams_of[0], (BATCH_COUNT, SEQUENCE_LENGTH, WINDOW_HEADS * E), 1.0, 6.0, ((0, 8), (1, 64)))
    keys = normal_values(streams_of[1], (BATCH_COUNT, SEQUENCE_LENGTH, WINDOW_HEADS * E), 1.0, 6.0, ((0, 8), (1, 64)))
    values = normal_values(streams_of[2], (BATCH_COUNT, SEQUENCE_LENGTH, WINDOW_HEADS * E), 1.0, 6.0, ((0, 8), (1, 64)))
    log_decay = draw_log_decay(jax.random.fold_in(streams_of[6], 71), 0)
    gain = jnp.clip(1.0 + 0.18 * jax.random.normal(streams_of[4], (WINDOW_HEADS * E,), jnp.float32), 0.1, 1.9)
    out_grad = bell_draw_with(streams_of[5], (BATCH_COUNT, SEQUENCE_LENGTH, WINDOW_HEADS * E), 1.0, 16.0, ((0, 8), (1, 64)), (1, 2, 64, 4.0))
    return dict(queries=queries, keys=keys, values=values, log_decay=log_decay, gain=gain, out_grad=out_grad)


EPSILON = 1e-06

def round_half(tensor):
    return lax.optimization_barrier(tensor.astype(jnp.bfloat16)).astype(jnp.float32)

def split_heads(block):
    length = block.shape[0]
    return block.astype(jnp.float32).reshape(length, WINDOW_HEADS, E)

def causal_decay(cumulative):
    length = cumulative.shape[-1]
    causal = jnp.tril(jnp.ones((length, length), dtype=bool))
    spread = cumulative[..., :, None] - cumulative[..., None, :]
    return jnp.where(causal, jnp.exp(jnp.where(causal, spread, 0.0)), 0.0)

def local_terms(query_block, key_block, decay_block):
    query_heads = split_heads(query_block)
    key_heads = split_heads(key_block)
    cumulative = jnp.cumsum(decay_block, axis=1)
    from_start = jnp.exp(cumulative).T[:, :, None]
    to_end = jnp.exp(cumulative[:, -1:] - cumulative).T[:, :, None]
    decay_mask = causal_decay(cumulative)
    weights = round_half(jnp.einsum('thi,shi->hts', query_heads, key_heads) * decay_mask)
    return (query_heads, key_heads, cumulative, from_start, to_end, decay_mask, weights)

def summarize(packed):
    key_block, value_block, decay_block = packed
    cumulative = jnp.cumsum(decay_block, axis=1)
    to_end = jnp.exp(cumulative[:, -1:] - cumulative).T[:, :, None]
    key_decayed = round_half(split_heads(key_block) * to_end)
    block_state = jnp.einsum('thi,thj->hij', key_decayed, split_heads(value_block))
    return (block_state, jnp.exp(cumulative[:, -1]))

def carry_forward(states, decays):

    def advance(carried, packed):
        block_state, block_decay = packed
        return (block_decay[:, None, None] * carried + block_state, carried)
    _, entering = lax.scan(advance, jnp.zeros_like(states[0]), (states, decays))
    return entering

def carry_backward(adjoints, decays):

    def advance(carried, packed):
        block_adjoint, block_decay = packed
        return (block_decay[:, None, None] * carried + block_adjoint, carried)
    _, returned = lax.scan(advance, jnp.zeros_like(adjoints[0]), (adjoints, decays), reverse=True)
    return returned

def reference(queries, keys, values, log_decay, gain, out_grad):
    blocks = SEQUENCE_LENGTH // TOK_DEV
    full_width = WINDOW_HEADS * E
    gain_heads = gain.astype(jnp.float32).reshape(WINDOW_HEADS, E)

    def split_rows(tensor):
        return tensor.reshape(BATCH_COUNT * blocks, TOK_DEV, full_width)
    query_rows = split_rows(queries)
    key_rows = split_rows(keys)
    value_rows = split_rows(values)
    grad_rows = split_rows(out_grad)
    decay_rows = log_decay.reshape(BATCH_COUNT, WINDOW_HEADS, blocks, TOK_DEV).transpose(0, 2, 1, 3).reshape(BATCH_COUNT * blocks, WINDOW_HEADS, TOK_DEV)
    states, decays = lax.map(summarize, (key_rows, value_rows, decay_rows))
    states = states.reshape(BATCH_COUNT, blocks, WINDOW_HEADS, E, E)
    decays = decays.reshape(BATCH_COUNT, blocks, WINDOW_HEADS)
    entering = jax.vmap(carry_forward)(states, decays).reshape(BATCH_COUNT * blocks, WINDOW_HEADS, E, E)

    def first_pass(packed):
        query_block, key_block, value_block, decay_block, grad_block, entering_block = packed
        query_heads, key_heads, cumulative, from_start, to_end, decay_mask, weights = local_terms(query_block, key_block, decay_block)
        value_heads = split_heads(value_block)
        entering_half = round_half(entering_block)
        attended = from_start * jnp.einsum('thi,hij->thj', query_heads, entering_half) + jnp.einsum('hts,shj->thj', weights, value_heads)
        root_mean = jnp.sqrt(lax.optimization_barrier(jnp.mean(attended * attended, axis=-1, keepdims=True)) + EPSILON)
        normed = attended / root_mean
        upstream = split_heads(grad_block)
        scaled_up = gain_heads * upstream
        attended_grad = round_half((scaled_up - normed * lax.optimization_barrier(jnp.mean(scaled_up * normed, axis=-1, keepdims=True))) / root_mean)
        gain_term = lax.optimization_barrier(jnp.sum(upstream * normed, axis=0))
        grad_weights = round_half(jnp.einsum('thj,shj->hts', attended_grad, value_heads) * decay_mask)
        query_grad = from_start * jnp.einsum('thj,hij->thi', attended_grad, entering_half) + jnp.einsum('hts,shi->thi', grad_weights, key_heads)
        query_decayed = round_half(query_heads * from_start)
        block_adjoint = jnp.einsum('thi,thj->hij', query_decayed, attended_grad)
        length = query_block.shape[0]
        return (query_grad.reshape(length, full_width).astype(jnp.bfloat16), attended_grad.astype(jnp.bfloat16), block_adjoint, gain_term)
    query_grads, grad_halves, adjoints, gain_terms = lax.map(first_pass, (query_rows, key_rows, value_rows, decay_rows, grad_rows, entering))
    returned = jax.vmap(carry_backward)(adjoints.reshape(BATCH_COUNT, blocks, WINDOW_HEADS, E, E), decays).reshape(BATCH_COUNT * blocks, WINDOW_HEADS, E, E)

    def second_pass(packed):
        query_block, key_block, value_block, decay_block, grad_half, returned_block = packed
        query_heads, key_heads, cumulative, from_start, to_end, decay_mask, weights = local_terms(query_block, key_block, decay_block)
        value_heads = split_heads(value_block)
        attended_grad = grad_half.astype(jnp.float32)
        grad_weights = round_half(jnp.einsum('thj,shj->hts', attended_grad, value_heads) * decay_mask)
        returned_half = round_half(returned_block)
        key_grad = to_end * jnp.einsum('thj,hij->thi', value_heads, returned_half) + jnp.einsum('hts,thi->shi', grad_weights, query_heads)
        value_grad = to_end * jnp.einsum('thi,hij->thj', key_heads, returned_half) + jnp.einsum('hts,thj->shj', weights, attended_grad)
        length = query_block.shape[0]
        return (key_grad.reshape(length, full_width).astype(jnp.bfloat16), value_grad.reshape(length, full_width).astype(jnp.bfloat16))
    key_grads, value_grads = lax.map(second_pass, (query_rows, key_rows, value_rows, decay_rows, grad_halves, returned))
    gain_grad = lax.optimization_barrier(jnp.sum(gain_terms, axis=0)).reshape(full_width)
    return (query_grads.reshape(BATCH_COUNT, SEQUENCE_LENGTH, full_width), key_grads.reshape(BATCH_COUNT, SEQUENCE_LENGTH, full_width), value_grads.reshape(BATCH_COUNT, SEQUENCE_LENGTH, full_width), gain_grad)
```

```python
import functools

import jax
import jax.numpy as jnp
from jax import lax
from jax.experimental import pallas as pl
from jax.experimental.pallas import tpu as pltpu
from jax.sharding import PartitionSpec as P

EPSILON = 1e-06
HEADS = 8
E = 128
NX = 4
PER = HEADS // NX
AWAY = (2, 1, 3)
NEAR = (0, 1, 3, 2)
F32 = jnp.float32
BF16 = jnp.bfloat16
MESH = pl.DeviceIdType.MESH


def dot(a, b, ca, cb):
    return lax.dot_general(a, b, (((ca,), (cb,)), ((), ())), preferred_element_type=F32)


def kernel(nz, nd, q, k, v, ld, gain, og, qg, kg, vg, gg,
           fs, te, dm, wts, att, ag, kgi, vgi,
           dself, dx, drow, dz, st, xr, rt, zr, zp, zb, ex, eb,
           gt, gx, gxs, gz, gzs, gd,
           xs_s, xs_r, zs_s, zs_r, zb_s, zb_r, xb_s, xb_r,
           dx_s, dx_r, dz_s, dz_r, gd_s, gx_r, gz_r, gd_r):
    ch = E // nz
    c = lax.axis_index("ctx")
    me = lax.axis_index("dp")
    z = lax.div(c, NX)
    x = lax.rem(c, NX)

    def xat(n):
        return lax.rem(x + n, NX)

    def zat(n):
        return lax.rem(z + n, nz)

    def dat(n):
        return lax.rem(me + n, nd)

    def xdev(i):
        return {"ctx": z * NX + i}

    def zdev(i):
        return {"ctx": i * NX + x}

    def ddev(i):
        return {"dp": i}

    def rcopy(src, dst, ss, rs, dev):
        return pltpu.make_async_remote_copy(
            src_ref=src, dst_ref=dst, send_sem=ss, recv_sem=rs, device_id=dev, device_id_type=MESH
        )

    def each(count, f):
        def one(i, carry):
            f(i)
            return carry

        lax.fori_loop(1, count, one, 0)

    def rows(i):
        return pl.ds(pl.multiple_of(i * ch, ch), ch)

    def cols(h):
        return pl.ds(h * E if isinstance(h, int) else pl.multiple_of(h * E, E), E)

    barrier = pltpu.get_barrier_semaphore()
    for n in range(1, NX):
        pl.semaphore_signal(barrier, inc=1, device_id=xdev(xat(n)), device_id_type=MESH)
    each(nz, lambda i: pl.semaphore_signal(barrier, inc=1, device_id=zdev(zat(i)), device_id_type=MESH))
    each(nd, lambda i: pl.semaphore_signal(barrier, inc=1, device_id=ddev(dat(i)), device_id_type=MESH))

    first = lax.broadcasted_iota(jnp.int32, (E, E), 0)
    second = lax.broadcasted_iota(jnp.int32, (E, E), 1)
    upper = jnp.where(first <= second, 1.0, 0.0).astype(F32)
    causal = second <= first
    cum = lax.dot_general(
        ld[...], upper, (((1,), (0,)), ((), ())),
        precision=lax.Precision.HIGHEST, preferred_element_type=F32,
    )
    end = cum[:, E - 1:E]
    dself[...] = jnp.exp(jnp.broadcast_to(end, (HEADS, E)))
    cum_col = cum.T
    fs_col = jnp.exp(cum).T
    te_col = jnp.exp(end - cum).T
    for h in range(HEADS):
        fs[h] = jnp.broadcast_to(fs_col[:, h:h + 1], (E, E))
        te[h] = jnp.broadcast_to(te_col[:, h:h + 1], (E, E))

    for j in range(PER):
        for n in (2, 1, 3, 0):
            h = PER * xat(n) + j
            kd = (k[:, cols(h)].astype(F32) * te[h]).astype(BF16)
            state = dot(kd, v[:, cols(h)], 0, 0)
            if n:
                st[0, h] = state
            else:
                xr[0, j, x] = state
    dx[x] = dself[...]

    pl.semaphore_wait(barrier, NX - 1 + nz - 1 + nd - 1)

    def dx_copy(i, slot):
        return rcopy(dself, dx.at[slot], dx_s.at[i], dx_r.at[slot], xdev(i))

    def dz_copy(i, slot):
        return rcopy(drow, dz.at[slot], dz_s.at[i], dz_r.at[slot], zdev(i))

    def xs_copy(d, j, i, slot):
        return rcopy(st.at[d, PER * i + j], xr.at[d, j, slot], xs_s.at[j, i], xs_r.at[d, j, slot], xdev(i))

    def zs_copy(d, j, i, slot):
        return rcopy(rt.at[d, j, rows(i)], zr.at[d, j, slot], zs_s.at[j, i], zs_r.at[d, j, slot], zdev(i))

    def zb_copy(d, j, i, slot):
        return rcopy(zp.at[d, j, i], zb.at[d, j, rows(slot)], zb_s.at[j, i], zb_r.at[d, j, slot], zdev(i))

    def xb_copy(d, j, i, slot):
        return rcopy(
            ex.at[d, j, i], eb.at[d, PER * slot + j], xb_s.at[j, i], xb_r.at[d, j, slot], xdev(i)
        )

    def gx_copy(i, slot):
        return rcopy(gt, gx.at[slot], dx_s.at[i], gx_r.at[slot], xdev(i))

    def gz_copy(i, slot):
        return rcopy(gxs, gz.at[slot], dz_s.at[i], gz_r.at[slot], zdev(i))

    def gd_copy(i, slot):
        return rcopy(gzs, gd.at[slot], gd_s.at[i], gd_r.at[slot], ddev(i))

    for n in AWAY:
        dx_copy(xat(n), x).start()
    for j in range(PER):
        for n in AWAY:
            xs_copy(0, j, xat(n), x).start()

    def scan(d, fill):
        steps = range(NX) if d == 0 else range(NX - 1, -1, -1)
        for j in range(PER):
            for n in (1, 3, 2):
                xs_copy(d, j, xat(n), xat(n)).wait_recv()
            total = None
            for i in steps:
                part = xr[d, j, i]
                if total is None:
                    total = part
                else:
                    total = dx[i, pl.ds(PER * x + j, 1), :] * total + part
            rt[d, j] = total
            zr[d, j, z] = rt[d, j, rows(z)]
            each(nz, lambda i: zs_copy(d, j, zat(i), z).start())
            fill()
        for j in range(PER):
            each(nz, lambda i: zs_copy(d, j, zat(i), zat(i)).wait_recv())
            run = jnp.zeros((ch, E), F32)
            for s in range(nz):
                i = s if d == 0 else nz - 1 - s
                zp[d, j, i] = run
                if s < nz - 1:
                    run = dz[i, pl.ds(PER * x + j, 1), :] * run + zr[d, j, i]
            zb[d, j, rows(z)] = zp[d, j, z]
            each(nz, lambda i: zb_copy(d, j, zat(i), z).start())
            fill()
        for j in range(PER):
            each(nz, lambda i: zb_copy(d, j, zat(i), zat(i)).wait_recv())
            carried = zb[d, j]
            for s, i in enumerate(steps):
                ex[d, j, i] = carried
                if s < NX - 1:
                    carried = dx[i, pl.ds(PER * x + j, 1), :] * carried + xr[d, j, i]
            for n in AWAY:
                xb_copy(d, j, xat(n), x).start()
            eb[d, PER * x + j] = ex[d, j, x]

    def early(h):
        own = cum_col[:, h:h + 1] - cum[h:h + 1, :]
        mask = jnp.where(causal, jnp.exp(jnp.where(causal, own, 0.0)), 0.0)
        dm[h] = mask
        w = (dot(q[:, cols(h)], k[:, cols(h)], 1, 1) * mask).astype(BF16)
        wts[h] = w
        att[h] = dot(w, v[:, cols(h)], 1, 0)

    early(0)
    for n in AWAY:
        dx_copy(xat(n), xat(n)).wait_recv()
    drow[...] = dx[0] * dx[1] * dx[2] * dx[3]
    dz[z] = drow[...]
    each(nz, lambda i: dz_copy(zat(i), z).start())
    early(1)
    todo = [(2, 3), (4, 5), (6,), (7,)]

    def fill_early():
        for h in todo.pop(0):
            early(h)
        if len(todo) == 2:
            each(nz, lambda i: dz_copy(zat(i), zat(i)).wait_recv())

    scan(0, fill_early)

    for n in AWAY:
        dx_copy(xat(n), x).wait_send()
    each(nz, lambda i: dz_copy(zat(i), z).wait_send())
    for j in range(PER):
        for n in AWAY:
            xs_copy(0, j, xat(n), x).wait_send()
        each(nz, lambda i: zs_copy(0, j, zat(i), z).wait_send())
        each(nz, lambda i: zb_copy(0, j, zat(i), z).wait_send())

    for j in range(PER):
        for n in NEAR:
            i = xat(n)
            h = PER * i + j
            if n:
                xb_copy(0, j, i, i).wait_recv()
            eh = eb[0, h].astype(BF16)
            qh = q[:, cols(h)]
            start = fs[h]
            attended = start * dot(qh, eh, 1, 0) + att[h]
            inverse = lax.rsqrt(jnp.mean(attended * attended, axis=-1, keepdims=True) + EPSILON)
            normed = attended * inverse
            up = og[:, cols(h)].astype(F32)
            scaled = gain[pl.ds(h, 1), :] * up
            a = (
                (scaled - normed * jnp.mean(scaled * normed, axis=-1, keepdims=True)) * inverse
            ).astype(BF16)
            ag[h] = a
            qd = (qh.astype(F32) * start).astype(BF16)
            adjoint = dot(qd, a, 0, 0)
            if n:
                st[1, h] = adjoint
                xs_copy(1, j, i, x).start()
            else:
                xr[1, j, x] = adjoint
            gt[pl.ds(h, 1), :] = jnp.sum(up * normed, axis=0, keepdims=True)
    for n in AWAY:
        gx_copy(xat(n), x).start()
    gx[x] = gt[...]

    def late(h):
        a = ag[h]
        vh = v[:, cols(h)]
        gw = (dot(a, vh, 1, 1) * dm[h]).astype(BF16)
        eh = eb[0, h].astype(BF16)
        grad = fs[h] * dot(a, eh, 1, 1) + dot(gw, k[:, cols(h)], 1, 0)
        qg[:, cols(h)] = grad.astype(BF16)
        kgi[h] = dot(gw, q[:, cols(h)], 0, 0)
        vgi[h] = dot(wts[h], a, 0, 0)

    late(0)
    late(1)
    rest = [(2, 3), (4, 5), (6,), (7,)]

    def fill_late():
        for h in rest.pop(0):
            late(h)
        if len(rest) == 2:
            for n in AWAY:
                gx_copy(xat(n), xat(n)).wait_recv()
            gxs[...] = gx[0] + gx[1] + gx[2] + gx[3]
            each(nz, lambda i: gz_copy(zat(i), z).start())
            gz[z] = gxs[...]
        if len(rest) == 0:
            each(nz, lambda i: gz_copy(zat(i), zat(i)).wait_recv())
            gzs[...] = jnp.sum(gz[...], axis=0)
            each(nd, lambda i: gd_copy(dat(i), me).start())
            gd[me] = gzs[...]

    for j in range(PER):
        for n in AWAY:
            xb_copy(0, j, xat(n), x).wait_send()

    scan(1, fill_late)

    for j in range(PER):
        for n in NEAR:
            i = xat(n)
            h = PER * i + j
            if n:
                xb_copy(1, j, i, i).wait_recv()
            rh = eb[1, h].astype(BF16)
            stop = te[h]
            kg[:, cols(h)] = (stop * dot(v[:, cols(h)], rh, 1, 1) + kgi[h]).astype(BF16)
            vg[:, cols(h)] = (stop * dot(k[:, cols(h)], rh, 1, 0) + vgi[h]).astype(BF16)

    each(nd, lambda i: gd_copy(dat(i), dat(i)).wait_recv())
    gg[...] = jnp.sum(gd[...], axis=0)

    for n in AWAY:
        gx_copy(xat(n), x).wait_send()
    each(nz, lambda i: gz_copy(zat(i), z).wait_send())
    each(nd, lambda i: gd_copy(dat(i), me).wait_send())
    for j in range(PER):
        for n in AWAY:
            xs_copy(1, j, xat(n), x).wait_send()
            xb_copy(1, j, xat(n), x).wait_send()
        each(nz, lambda i: zs_copy(1, j, zat(i), z).wait_send())
        each(nz, lambda i: zb_copy(1, j, zat(i), z).wait_send())


def body(queries, keys, values, log_decay, gain, out_grad):
    nc = lax.axis_size("ctx")
    nd = lax.axis_size("dp")
    nz = nc // NX
    ch = E // nz
    width = HEADS * E

    def vm(*shape, dtype=F32):
        return pltpu.VMEM(shape, dtype)

    dma = lambda *shape: pltpu.SemaphoreType.DMA(shape)
    flat = lambda a: a.reshape(E, width)
    wide = jax.ShapeDtypeStruct((E, width), BF16)
    qg, kg, vg, gg = pl.pallas_call(
        functools.partial(kernel, nz, nd),
        out_shape=(wide, wide, wide, jax.ShapeDtypeStruct((HEADS, E), F32)),
        in_specs=[pl.BlockSpec(memory_space=pltpu.VMEM)] * 6,
        out_specs=tuple([pl.BlockSpec(memory_space=pltpu.VMEM)] * 4),
        scratch_shapes=[
            vm(HEADS, E, E), vm(HEADS, E, E), vm(HEADS, E, E),
            vm(HEADS, E, E, dtype=BF16), vm(HEADS, E, E), vm(HEADS, E, E, dtype=BF16),
            vm(HEADS, E, E), vm(HEADS, E, E),
            vm(HEADS, E), vm(NX, HEADS, E), vm(HEADS, E), vm(nz, HEADS, E),
            vm(2, HEADS, E, E), vm(2, PER, NX, E, E), vm(2, PER, E, E),
            vm(2, PER, nz, ch, E), vm(2, PER, nz, ch, E), vm(2, PER, E, E),
            vm(2, PER, NX, E, E), vm(2, HEADS, E, E),
            vm(HEADS, E), vm(NX, HEADS, E), vm(HEADS, E), vm(nz, HEADS, E),
            vm(HEADS, E), vm(nd, HEADS, E),
            dma(PER, NX), dma(2, PER, NX), dma(PER, nz), dma(2, PER, nz),
            dma(PER, nz), dma(2, PER, nz), dma(PER, NX), dma(2, PER, NX),
            dma(NX), dma(NX), dma(nz), dma(nz), dma(nd), dma(NX), dma(nz), dma(nd),
        ],
        compiler_params=pltpu.CompilerParams(
            collective_id=0, has_side_effects=True, vmem_limit_bytes=48 * 1024 * 1024
        ),
    )(
        flat(queries), flat(keys), flat(values), log_decay.reshape(HEADS, E),
        gain.reshape(HEADS, E), flat(out_grad),
    )
    portion = width // nc
    share = lax.dynamic_slice_in_dim(gg.reshape(width), lax.axis_index("ctx") * portion, portion)
    whole = lambda a: a.reshape(1, E, width)
    return whole(qg), whole(kg), whole(vg), share


def solution(mesh):
    in_specs = (
        P("dp", "ctx", None),
        P("dp", "ctx", None),
        P("dp", "ctx", None),
        P("dp", None, "ctx"),
        P(),
        P("dp", "ctx", None),
    )
    out_specs = (P("dp", "ctx", None), P("dp", "ctx", None), P("dp", "ctx", None), P("ctx"))
    return jax.shard_map(body, mesh=mesh, in_specs=in_specs, out_specs=out_specs, check_vma=False)
```

```python
import functools

import jax
import jax.numpy as jnp
from jax import lax
from jax.experimental import pallas as pl
from jax.experimental.pallas import tpu as pltpu
from jax.sharding import PartitionSpec as P

EPSILON = 1e-06
HEADS = 8
E = 128
NX = 4
HALF = E // 2
PER = HEADS // NX
AWAY = (2, 1, 3)
NEAR = (0, 1, 3, 2)
F32 = jnp.float32
BF16 = jnp.bfloat16
MESH = pl.DeviceIdType.MESH


def dot(a, b, ca, cb):
    return lax.dot_general(a, b, (((ca,), (cb,)), ((), ())), preferred_element_type=F32)


def kernel(nz, nd, qi, ki, vi, ldi, gaini, ogi, qg, kg, vg, gg, q, k, v, og, ld, gain,
           fs, te, dm, wts, att, ag, kgi, vgi,
           dself, dx, drow, dz, st, xr, rt, zr, zp, zb, ex, eb,
           gt, gx, gxs, gz, gzs, gd,
           xs_s, xs_r, zs_s, zs_r, zb_s, zb_r, xb_s, xb_r,
           dx_s, dx_r, dz_s, dz_r, gd_s, gx_r, gz_r, gd_r, in_s):
    ch = E // nz
    c = lax.axis_index("ctx")
    me = lax.axis_index("dp")
    z = lax.div(c, NX)
    x = lax.rem(c, NX)

    def xat(n):
        return lax.rem(x + n, NX)

    def zat(n):
        return lax.rem(z + n, nz)

    def dat(n):
        return lax.rem(me + n, nd)

    def xdev(i):
        return {"ctx": z * NX + i}

    def zdev(i):
        return {"ctx": i * NX + x}

    def ddev(i):
        return {"dp": i}

    def rcopy(src, dst, ss, rs, dev):
        return pltpu.make_async_remote_copy(
            src_ref=src, dst_ref=dst, send_sem=ss, recv_sem=rs, device_id=dev, device_id_type=MESH
        )

    def each(count, f):
        def one(i, carry):
            f(i)
            return carry

        lax.fori_loop(1, count, one, 0)

    def far(f):
        def one(i, carry):
            f(zat(nz // 2 + ((i + 1) // 2) * (1 - 2 * (i % 2))))
            return carry

        lax.fori_loop(0, nz - 1, one, 0)

    def owners(p, f):
        def one(i, carry):
            near = (i + 1) // 2
            f(zat(nz // 2 + 2 * near * (1 - 2 * (i % 2)) + nz))
            return carry

        def other(i, carry):
            near = 2 * (i // 2) + 1
            f(zat(nz // 2 + near * (1 - 2 * (i % 2)) + nz))
            return carry

        same = (z + p + nz // 2) % 2 == 0

        @pl.when(same)
        def _():
            lax.fori_loop(0, nz // 2 - (1 if nz // 2 % 2 == 0 else 0), one, 0)

        @pl.when(jnp.logical_not(same))
        def _():
            lax.fori_loop(0, nz // 2 - (1 if nz // 2 % 2 else 0), other, 0)

    def rows(i):
        return pl.ds(pl.multiple_of(((i % 2) * (nz // 2) + i // 2) * ch, ch), ch)

    def half(p):
        return pl.ds(p * HALF, HALF)

    def bulk(ref, sem):
        return rcopy(ref, ref, sem, sem, xdev(xat(1)))

    def cols(h):
        return pl.ds(h * E if isinstance(h, int) else pl.multiple_of(h * E, E), E)

    loads = [
        pltpu.make_async_copy(a, b, in_s.at[i])
        for i, (a, b) in enumerate(((ki, k), (vi, v), (qi, q), (ogi, og), (ldi, ld), (gaini, gain)))
    ]
    for i in (4, 0, 1, 2, 3, 5):
        loads[i].start()
    barrier = pltpu.get_barrier_semaphore()
    for n in range(1, NX):
        pl.semaphore_signal(barrier, inc=1, device_id=xdev(xat(n)), device_id_type=MESH)
    each(nz, lambda i: pl.semaphore_signal(barrier, inc=1, device_id=zdev(zat(i)), device_id_type=MESH))
    each(nd, lambda i: pl.semaphore_signal(barrier, inc=1, device_id=ddev(dat(i)), device_id_type=MESH))

    first = lax.broadcasted_iota(jnp.int32, (E, E), 0)
    second = lax.broadcasted_iota(jnp.int32, (E, E), 1)
    upper = jnp.where(first <= second, 1.0, 0.0).astype(F32)
    causal = second <= first
    loads[4].wait()
    cum = lax.dot_general(
        ld[...], upper, (((1,), (0,)), ((), ())),
        precision=lax.Precision.HIGHEST, preferred_element_type=F32,
    )
    end = cum[:, E - 1:E]
    dself[...] = jnp.exp(jnp.broadcast_to(end, (HEADS, E)))
    cum_col = cum.T
    fs_col = jnp.exp(cum).T
    te_col = jnp.exp(end - cum).T
    for h in range(HEADS):
        fs[h] = jnp.broadcast_to(fs_col[:, h:h + 1], (E, E))
        te[h] = jnp.broadcast_to(te_col[:, h:h + 1], (E, E))

    loads[0].wait()
    loads[1].wait()
    for j in range(PER):
        for n in (2, 1, 3, 0):
            h = PER * xat(n) + j
            kd = (k[:, cols(h)].astype(F32) * te[h]).astype(BF16)
            state = dot(kd, v[:, cols(h)], 0, 0)
            if n:
                st[0, h] = state
            else:
                xr[0, j, x] = state
    dx[x] = dself[...]

    pl.semaphore_wait(barrier, NX - 1 + nz - 1 + nd - 1)

    def dx_copy(i, slot):
        return rcopy(dself, dx.at[slot], dx_s.at[i], dx_r.at[slot], xdev(i))

    def dz_copy(i, slot):
        return rcopy(drow, dz.at[slot], dz_s.at[0], dz_r.at[0], zdev(i))

    def xs_copy(d, j, p, i, slot):
        return rcopy(
            st.at[d, PER * i + j, half(p)], xr.at[d, j, slot, half(p)],
            xs_s.at[j, p, i], xs_r.at[d, j, p, slot], xdev(i),
        )

    def zs_copy(d, j, i, slot):
        return rcopy(rt.at[d, j, rows(i)], zr.at[d, j, slot], zs_s.at[d, j], zs_r.at[d, j], zdev(i))

    def zb_copy(d, j, i, slot):
        return rcopy(zp.at[d, j, i], zb.at[d, j, rows(slot)], zb_s.at[d, j], zb_r.at[d, j], zdev(i))

    def xb_copy(d, j, p, i, slot):
        return rcopy(
            ex.at[d, j, i, half(p)], eb.at[d, PER * slot + j, half(p)],
            xb_s.at[j, p, i], xb_r.at[d, j, p, slot], xdev(i),
        )

    def gx_copy(i, slot):
        return rcopy(gt, gx.at[slot], dx_s.at[i], gx_r.at[slot], xdev(i))

    def gz_copy(i, slot):
        return rcopy(gxs.at[pl.ds(i // (nz // HEADS), 1)] if nz >= HEADS else gxs.at[pl.ds(i * (HEADS // nz), 1)],
                     gz.at[slot], dz_s.at[1], gz_r.at[0], zdev(i))

    def gd_copy(i, slot):
        return rcopy(gzs, gd.at[slot], gd_s.at[0], gd_r.at[0], ddev(i))

    for n in AWAY:
        dx_copy(xat(n), x).start()
    for j in range(PER):
        for p in range(2):
            for n in AWAY:
                xs_copy(0, j, p, xat(n), x).start()

    def decay(i, j):
        return dx[i, pl.ds(PER * x + j, 1), :]

    def scan(d, fill):
        steps = range(NX) if d == 0 else range(NX - 1, -1, -1)
        for j in range(PER):
            for p in range(2):
                for n in (1, 3, 2):
                    xs_copy(d, j, p, xat(n), xat(n)).wait_recv()
                total = None
                for i in steps:
                    part = xr[d, j, i, half(p)]
                    total = part if total is None else decay(i, j) * total + part
                rt[d, j, half(p)] = total
                owners(p, lambda i: zs_copy(d, j, i, z).start())
            zr[d, j, z] = rt[d, j, rows(z)]
            fill()
        for j in range(PER):
            bulk(zr.at[d, j, pl.ds(0, nz - 1)], zs_r.at[d, j]).wait_recv()
            run = jnp.zeros((ch, E), F32)
            for s in range(nz):
                i = s if d == 0 else nz - 1 - s
                zp[d, j, i] = run
                if s < nz - 1:
                    run = dz[i, j:j + 1, :] * run + zr[d, j, i]
            far(lambda i: zb_copy(d, j, i, z).start())
            zb[d, j, rows(z)] = zp[d, j, z]
            fill()
        for j in range(PER):
            bulk(zb.at[d, j, pl.ds(0, (nz - 1) * ch)], zb_r.at[d, j]).wait_recv()
            for p in range(2):
                carried = zb[d, j, half(p)]
                for s, i in enumerate(steps):
                    ex[d, j, i, half(p)] = carried
                    if s < NX - 1:
                        carried = decay(i, j) * carried + xr[d, j, i, half(p)]
                for n in AWAY:
                    xb_copy(d, j, p, xat(n), x).start()
            eb[d, PER * x + j] = ex[d, j, x]

    def sent(d):
        for j in range(PER):
            for p in range(2):
                for n in AWAY:
                    xs_copy(d, j, p, xat(n), x).wait_send()
                    xb_copy(d, j, p, xat(n), x).wait_send()
            bulk(rt.at[d, j, pl.ds(0, (nz - 1) * ch)], zs_s.at[d, j]).wait_send()
            bulk(zp.at[d, j, pl.ds(0, nz - 1)], zb_s.at[d, j]).wait_send()

    def early(h):
        own = cum_col[:, h:h + 1] - cum[h:h + 1, :]
        mask = jnp.where(causal, jnp.exp(jnp.where(causal, own, 0.0)), 0.0)
        dm[h] = mask
        w = (dot(q[:, cols(h)], k[:, cols(h)], 1, 1) * mask).astype(BF16)
        wts[h] = w
        att[h] = dot(w, v[:, cols(h)], 1, 0)

    loads[2].wait()
    early(0)
    for n in AWAY:
        dx_copy(xat(n), xat(n)).wait_recv()
    for j in range(PER):
        drow[j:j + 1, :] = decay(0, j) * decay(1, j) * decay(2, j) * decay(3, j)
    dz[z] = drow[...]
    far(lambda i: dz_copy(i, z).start())
    early(1)
    todo = [(2, 3), (4, 5), (6,), (7,)]

    def fill_early():
        for h in todo.pop(0):
            early(h)
        if len(todo) == 2:
            bulk(dz.at[pl.ds(0, nz - 1)], dz_r.at[0]).wait_recv()

    scan(0, fill_early)

    loads[3].wait()
    loads[5].wait()
    for n in AWAY:
        dx_copy(xat(n), x).wait_send()
    for j in range(PER):
        for p in range(2):
            for n in AWAY:
                xs_copy(0, j, p, xat(n), x).wait_send()

    for j in range(PER):
        for n in NEAR:
            i = xat(n)
            h = PER * i + j
            if n:
                for p in range(2):
                    xb_copy(0, j, p, i, i).wait_recv()
            eh = eb[0, h].astype(BF16)
            qh = q[:, cols(h)]
            start = fs[h]
            attended = start * dot(qh, eh, 1, 0) + att[h]
            inverse = lax.rsqrt(jnp.mean(attended * attended, axis=-1, keepdims=True) + EPSILON)
            normed = attended * inverse
            up = og[:, cols(h)].astype(F32)
            scaled = gain[pl.ds(h, 1), :] * up
            a = (
                (scaled - normed * jnp.mean(scaled * normed, axis=-1, keepdims=True)) * inverse
            ).astype(BF16)
            ag[h] = a
            qd = (qh.astype(F32) * start).astype(BF16)
            adjoint = dot(qd, a, 0, 0)
            if n:
                st[1, h] = adjoint
                for p in range(2):
                    xs_copy(1, j, p, i, x).start()
            else:
                xr[1, j, x] = adjoint
            gt[pl.ds(h, 1), :] = jnp.sum(up * normed, axis=0, keepdims=True)
    for n in AWAY:
        gx_copy(xat(n), x).start()
    gx[x] = gt[...]

    def late(h):
        a = ag[h]
        vh = v[:, cols(h)]
        gw = (dot(a, vh, 1, 1) * dm[h]).astype(BF16)
        eh = eb[0, h].astype(BF16)
        grad = fs[h] * dot(a, eh, 1, 1) + dot(gw, k[:, cols(h)], 1, 0)
        qg[:, cols(h)] = grad.astype(BF16)
        kgi[h] = dot(gw, q[:, cols(h)], 0, 0)
        vgi[h] = dot(wts[h], a, 0, 0)

    late(0)
    late(1)
    rest = [(2, 3), (4, 5), (6,), (7,)]

    def fill_late():
        for h in rest.pop(0):
            late(h)
        if len(rest) == 2:
            for n in AWAY:
                gx_copy(xat(n), xat(n)).wait_recv()
            gxs[...] = gx[0] + gx[1] + gx[2] + gx[3]
            far(lambda i: gz_copy(i, z).start())
            gz[z] = gxs[pl.ds(z // (nz // HEADS), 1), :] if nz >= HEADS else gxs[pl.ds(z * (HEADS // nz), 1), :]
        if len(rest) == 0:
            bulk(gz.at[pl.ds(0, nz - 1)], gz_r.at[0]).wait_recv()
            gzs[...] = jnp.sum(gz[...], axis=0)
            each(nd, lambda i: gd_copy(dat(i), me).start())
            gd[me] = gzs[...]

    for j in range(PER):
        for p in range(2):
            for n in AWAY:
                xb_copy(0, j, p, xat(n), x).wait_send()

    scan(1, fill_late)

    for j in range(PER):
        for n in NEAR:
            i = xat(n)
            h = PER * i + j
            if n:
                for p in range(2):
                    xb_copy(1, j, p, i, i).wait_recv()
            rh = eb[1, h].astype(BF16)
            stop = te[h]
            kg[:, cols(h)] = (stop * dot(v[:, cols(h)], rh, 1, 1) + kgi[h]).astype(BF16)
            vg[:, cols(h)] = (stop * dot(k[:, cols(h)], rh, 1, 0) + vgi[h]).astype(BF16)

    bulk(gd.at[pl.ds(0, nd - 1)], gd_r.at[0]).wait_recv()
    gg[...] = jnp.sum(gd[...], axis=0)

    for n in AWAY:
        gx_copy(xat(n), x).wait_send()
    bulk(dz.at[pl.ds(0, nz - 1)], dz_s.at[0]).wait_send()
    bulk(gz.at[pl.ds(0, nz - 1)], dz_s.at[1]).wait_send()
    bulk(gd.at[pl.ds(0, nd - 1)], gd_s.at[0]).wait_send()
    for j in range(PER):
        bulk(rt.at[0, j, pl.ds(0, (nz - 1) * ch)], zs_s.at[0, j]).wait_send()
        bulk(zp.at[0, j, pl.ds(0, nz - 1)], zb_s.at[0, j]).wait_send()
    sent(1)


def body(queries, keys, values, log_decay, gain, out_grad):
    nc = lax.axis_size("ctx")
    nd = lax.axis_size("dp")
    nz = nc // NX
    ch = E // nz
    width = HEADS * E

    def vm(*shape, dtype=F32):
        return pltpu.VMEM(shape, dtype)

    dma = lambda *shape: pltpu.SemaphoreType.DMA(shape)
    flat = lambda a: a.reshape(E, width)
    hbm = pltpu.HBM
    wide = jax.ShapeDtypeStruct((E, width), BF16)
    qg, kg, vg, gg = pl.pallas_call(
        functools.partial(kernel, nz, nd),
        out_shape=(wide, wide, wide, jax.ShapeDtypeStruct((1, E), F32)),
        in_specs=[pl.BlockSpec(memory_space=m) for m in [hbm] * 6],
        out_specs=tuple([pl.BlockSpec(memory_space=pltpu.VMEM)] * 4),
        scratch_shapes=[
            *[vm(E, width, dtype=BF16)] * 4, vm(HEADS, E), vm(HEADS, E),
            vm(HEADS, E, E), vm(HEADS, E, E), vm(HEADS, E, E),
            vm(HEADS, E, E, dtype=BF16), vm(HEADS, E, E), vm(HEADS, E, E, dtype=BF16),
            vm(HEADS, E, E), vm(HEADS, E, E),
            vm(HEADS, E), vm(NX, HEADS, E), vm(PER, E), vm(nz, PER, E),
            vm(2, HEADS, E, E), vm(2, PER, NX, E, E), vm(2, PER, E, E),
            vm(2, PER, nz, ch, E), vm(2, PER, nz, ch, E), vm(2, PER, E, E),
            vm(2, PER, NX, E, E), vm(2, HEADS, E, E),
            vm(HEADS, E), vm(NX, HEADS, E), vm(HEADS, E), vm(nz, 1, E),
            vm(1, E), vm(nd, 1, E),
            dma(PER, 2, NX), dma(2, PER, 2, NX), dma(2, PER), dma(2, PER),
            dma(2, PER), dma(2, PER), dma(PER, 2, NX), dma(2, PER, 2, NX),
            dma(NX), dma(NX), dma(2), dma(1), dma(1), dma(NX), dma(1), dma(1), dma(6),
        ],
        compiler_params=pltpu.CompilerParams(
            collective_id=0, has_side_effects=True, vmem_limit_bytes=48 * 1024 * 1024
        ),
    )(
        flat(queries), flat(keys), flat(values), log_decay.reshape(HEADS, E),
        gain.reshape(HEADS, E), flat(out_grad),
    )
    portion = width // nc
    share = lax.dynamic_slice_in_dim(
        gg.reshape(E), lax.axis_index("ctx") * portion % E, portion
    )
    whole = lambda a: a.reshape(1, E, width)
    return whole(qg), whole(kg), whole(vg), share


def solution(mesh):
    in_specs = (
        P("dp", "ctx", None),
        P("dp", "ctx", None),
        P("dp", "ctx", None),
        P("dp", None, "ctx"),
        P(),
        P("dp", "ctx", None),
    )
    out_specs = (P("dp", "ctx", None), P("dp", "ctx", None), P("dp", "ctx", None), P("ctx"))
    return jax.shard_map(body, mesh=mesh, in_specs=in_specs, out_specs=out_specs, check_vma=False)
```

```python
import functools

import jax
import jax.numpy as jnp
from jax import lax
from jax.experimental import pallas as pl
from jax.experimental.pallas import tpu as pltpu
from jax.sharding import PartitionSpec as P

EPSILON = 1e-06
HEADS = 8
E = 128
NX = 4
HALF = E // 2
PER = HEADS // NX
AWAY = (2, 1, 3)
NEAR = (0, 1, 3, 2)
F32 = jnp.float32
BF16 = jnp.bfloat16
MESH = pl.DeviceIdType.MESH


def dot(a, b, ca, cb):
    return lax.dot_general(a, b, (((ca,), (cb,)), ((), ())), preferred_element_type=F32)


def kernel(nz, nd, qi, ki, vi, ldi, gaini, ogi, qg, kg, vg, gg, q, k, v, og, ld, gain,
           fs, te, dm, wts, att, ag, kgi, vgi,
           dself, dx, drow, dz, st, xr, rt, zr, zp, zb, ex, eb,
           gt, gx, gxs, gz, gzs, gd,
           xs_s, xs_r, zs_s, zs_r, zb_s, zb_r, xb_s, xb_r,
           dx_s, dx_r, dz_s, dz_r, gd_s, gx_r, gz_r, gd_r, in_s, second_s, third_s):
    ch = E // nz
    c = lax.axis_index("ctx")
    me = lax.axis_index("dp")
    z = lax.div(c, NX)
    x = lax.rem(c, NX)

    def xat(n):
        return lax.rem(x + n, NX)

    def zat(n):
        return lax.rem(z + n, nz)

    def dat(n):
        return lax.rem(me + n, nd)

    def xdev(i):
        return {"ctx": z * NX + i}

    def zdev(i):
        return {"ctx": i * NX + x}

    def ddev(i):
        return {"dp": i}

    def rcopy(src, dst, ss, rs, dev):
        return pltpu.make_async_remote_copy(
            src_ref=src, dst_ref=dst, send_sem=ss, recv_sem=rs, device_id=dev, device_id_type=MESH
        )

    def each(count, f):
        def one(i, carry):
            f(i)
            return carry

        lax.fori_loop(1, count, one, 0)

    def far(f):
        def one(i, carry):
            f(zat(nz // 2 + ((i + 1) // 2) * (1 - 2 * (i % 2))))
            return carry

        lax.fori_loop(0, nz - 1, one, 0)

    def owners(p, f):
        def one(i, carry):
            near = (i + 1) // 2
            f(zat(nz // 2 + 2 * near * (1 - 2 * (i % 2)) + nz))
            return carry

        def other(i, carry):
            near = 2 * (i // 2) + 1
            f(zat(nz // 2 + near * (1 - 2 * (i % 2)) + nz))
            return carry

        same = (z + p + nz // 2) % 2 == 0

        @pl.when(same)
        def _():
            lax.fori_loop(0, nz // 2 - (1 if nz // 2 % 2 == 0 else 0), one, 0)

        @pl.when(jnp.logical_not(same))
        def _():
            lax.fori_loop(0, nz // 2 - (1 if nz // 2 % 2 else 0), other, 0)

    def rows(i):
        return pl.ds(pl.multiple_of(((i % 2) * (nz // 2) + i // 2) * ch, ch), ch)

    def half(p):
        return pl.ds(p * HALF, HALF)

    def bulk(ref, sem):
        return rcopy(ref, ref, sem, sem, xdev(xat(1)))

    def cols(h):
        return pl.ds(h * E if isinstance(h, int) else pl.multiple_of(h * E, E), E)

    loads = [
        pltpu.make_async_copy(a, b, in_s.at[i])
        for i, (a, b) in enumerate(((ki, k), (vi, v), (qi, q), (ogi, og), (ldi, ld), (gaini, gain)))
    ]
    for i in (4, 0, 1, 2, 3, 5):
        loads[i].start()
    barrier = pltpu.get_barrier_semaphore()
    for n in range(1, NX):
        pl.semaphore_signal(barrier, inc=1, device_id=xdev(xat(n)), device_id_type=MESH)
    for n in (1, 2, nz - 2, nz - 1):
        pl.semaphore_signal(barrier, inc=1, device_id=zdev(zat(n)), device_id_type=MESH)
    each(nd, lambda i: pl.semaphore_signal(barrier, inc=1, device_id=ddev(dat(i)), device_id_type=MESH))

    first = lax.broadcasted_iota(jnp.int32, (E, E), 0)
    second = lax.broadcasted_iota(jnp.int32, (E, E), 1)
    upper = jnp.where(first <= second, 1.0, 0.0).astype(F32)
    causal = second <= first
    loads[4].wait()
    cum = lax.dot_general(
        ld[...], upper, (((1,), (0,)), ((), ())),
        precision=lax.Precision.HIGHEST, preferred_element_type=F32,
    )
    end = cum[:, E - 1:E]
    dself[...] = jnp.exp(jnp.broadcast_to(end, (HEADS, E)))
    cum_col = cum.T
    fs_col = jnp.exp(cum).T
    te_col = jnp.exp(end - cum).T
    for h in range(HEADS):
        fs[h] = jnp.broadcast_to(fs_col[:, h:h + 1], (E, E))
        te[h] = jnp.broadcast_to(te_col[:, h:h + 1], (E, E))

    loads[0].wait()
    loads[1].wait()
    def dx_copy(i, slot):
        return rcopy(dself, dx.at[slot], dx_s.at[i], dx_r.at[slot], xdev(i))

    def dz_copy(i, slot):
        return rcopy(drow, dz.at[slot], dz_s.at[0], dz_r.at[0], zdev(i))

    def xs_copy(d, j, p, i, slot):
        return rcopy(
            st.at[d, PER * i + j, half(p)], xr.at[d, j, slot, half(p)],
            xs_s.at[j, p, i], xs_r.at[d, j, p, slot], xdev(i),
        )

    def zs_copy(d, j, i, slot):
        return rcopy(rt.at[d, j, rows(i)], zr.at[d, j, slot], zs_s.at[d, j], zs_r.at[d, j], zdev(i))

    def zb_copy(d, j, i, slot):
        return rcopy(zp.at[d, j, i], zb.at[d, j, rows(slot)], zb_s.at[d, j], zb_r.at[d, j], zdev(i))

    def xb_copy(d, j, p, i, slot):
        return rcopy(
            ex.at[d, j, i, half(p)], eb.at[d, PER * slot + j, half(p)],
            xb_s.at[j, p, i], xb_r.at[d, j, p, slot], xdev(i),
        )

    def gx_copy(i, slot):
        return rcopy(gt, gx.at[slot], dx_s.at[i], gx_r.at[slot], xdev(i))

    def gz_copy(i, slot):
        return rcopy(gxs.at[pl.ds(i // (nz // HEADS), 1)] if nz >= HEADS else gxs.at[pl.ds(i * (HEADS // nz), 1)],
                     gz.at[slot], dz_s.at[1], gz_r.at[0], zdev(i))

    def gd_copy(i, slot):
        return rcopy(gzs, gd.at[slot], gd_s.at[0], gd_r.at[0], ddev(i))

    def tell(sem, n):
        for m in (n, nz - n):
            pl.semaphore_signal(sem, inc=1, device_id=zdev(zat(m)), device_id_type=MESH)

    pl.semaphore_wait(barrier, NX - 1 + 4 + nd - 1)
    tell(second_s, 2)
    for n in AWAY:
        dx_copy(xat(n), x).start()
    dx[x] = dself[...]
    for j in range(PER):
        for n in (2, 1, 3, 0):
            h = PER * xat(n) + j
            kd = (k[:, cols(h)].astype(F32) * te[h]).astype(BF16)
            state = dot(kd, v[:, cols(h)], 0, 0)
            if n:
                st[0, h] = state
                for p in range(2):
                    xs_copy(0, j, p, xat(n), x).start()
            else:
                xr[0, j, x] = state
    pl.semaphore_wait(second_s, 2)
    if nz > 8:
        tell(third_s, 4)

    def decay(i, j):
        return dx[i, pl.ds(PER * x + j, 1), :]

    def scan(d, fill):
        steps = range(NX) if d == 0 else range(NX - 1, -1, -1)
        for j in range(PER):
            for p in range(2):
                for n in (1, 3, 2):
                    xs_copy(d, j, p, xat(n), xat(n)).wait_recv()
                total = None
                for i in steps:
                    part = xr[d, j, i, half(p)]
                    total = part if total is None else decay(i, j) * total + part
                rt[d, j, half(p)] = total
                owners(p, lambda i: zs_copy(d, j, i, z).start())
            zr[d, j, z] = rt[d, j, rows(z)]
            fill()
        for j in range(PER):
            bulk(zr.at[d, j, pl.ds(0, nz - 1)], zs_r.at[d, j]).wait_recv()
            run = jnp.zeros((ch, E), F32)
            for s in range(nz):
                i = s if d == 0 else nz - 1 - s
                zp[d, j, i] = run
                if s < nz - 1:
                    run = dz[i, j:j + 1, :] * run + zr[d, j, i]
            far(lambda i: zb_copy(d, j, i, z).start())
            zb[d, j, rows(z)] = zp[d, j, z]
            fill()
        for j in range(PER):
            bulk(zb.at[d, j, pl.ds(0, (nz - 1) * ch)], zb_r.at[d, j]).wait_recv()
            for p in range(2):
                carried = zb[d, j, half(p)]
                for s, i in enumerate(steps):
                    ex[d, j, i, half(p)] = carried
                    if s < NX - 1:
                        carried = decay(i, j) * carried + xr[d, j, i, half(p)]
                for n in AWAY:
                    xb_copy(d, j, p, xat(n), x).start()
            eb[d, PER * x + j] = ex[d, j, x]

    def sent(d):
        for j in range(PER):
            for p in range(2):
                for n in AWAY:
                    xs_copy(d, j, p, xat(n), x).wait_send()
                    xb_copy(d, j, p, xat(n), x).wait_send()
            bulk(rt.at[d, j, pl.ds(0, (nz - 1) * ch)], zs_s.at[d, j]).wait_send()
            bulk(zp.at[d, j, pl.ds(0, nz - 1)], zb_s.at[d, j]).wait_send()

    def early(h):
        own = cum_col[:, h:h + 1] - cum[h:h + 1, :]
        mask = jnp.where(causal, jnp.exp(jnp.where(causal, own, 0.0)), 0.0)
        dm[h] = mask
        w = (dot(q[:, cols(h)], k[:, cols(h)], 1, 1) * mask).astype(BF16)
        wts[h] = w
        att[h] = dot(w, v[:, cols(h)], 1, 0)

    loads[2].wait()
    early(0)
    for n in AWAY:
        dx_copy(xat(n), xat(n)).wait_recv()
    if nz > 8:
        pl.semaphore_wait(third_s, 2)
    for j in range(PER):
        drow[j:j + 1, :] = decay(0, j) * decay(1, j) * decay(2, j) * decay(3, j)
    dz[z] = drow[...]
    far(lambda i: dz_copy(i, z).start())
    early(1)
    todo = [(2, 3), (4, 5), (6,), (7,)]

    def fill_early():
        for h in todo.pop(0):
            early(h)
        if len(todo) == 2:
            bulk(dz.at[pl.ds(0, nz - 1)], dz_r.at[0]).wait_recv()

    scan(0, fill_early)

    loads[3].wait()
    loads[5].wait()
    for n in AWAY:
        dx_copy(xat(n), x).wait_send()
    for j in range(PER):
        for p in range(2):
            for n in AWAY:
                xs_copy(0, j, p, xat(n), x).wait_send()

    for j in range(PER):
        for n in NEAR:
            i = xat(n)
            h = PER * i + j
            if n:
                for p in range(2):
                    xb_copy(0, j, p, i, i).wait_recv()
            eh = eb[0, h].astype(BF16)
            qh = q[:, cols(h)]
            start = fs[h]
            attended = start * dot(qh, eh, 1, 0) + att[h]
            inverse = lax.rsqrt(jnp.mean(attended * attended, axis=-1, keepdims=True) + EPSILON)
            normed = attended * inverse
            up = og[:, cols(h)].astype(F32)
            scaled = gain[pl.ds(h, 1), :] * up
            a = (
                (scaled - normed * jnp.mean(scaled * normed, axis=-1, keepdims=True)) * inverse
            ).astype(BF16)
            ag[h] = a
            qd = (qh.astype(F32) * start).astype(BF16)
            adjoint = dot(qd, a, 0, 0)
            if n:
                st[1, h] = adjoint
                for p in range(2):
                    xs_copy(1, j, p, i, x).start()
            else:
                xr[1, j, x] = adjoint
            gt[pl.ds(h, 1), :] = jnp.sum(up * normed, axis=0, keepdims=True)
    for n in AWAY:
        gx_copy(xat(n), x).start()
    gx[x] = gt[...]

    def late(h):
        a = ag[h]
        vh = v[:, cols(h)]
        gw = (dot(a, vh, 1, 1) * dm[h]).astype(BF16)
        eh = eb[0, h].astype(BF16)
        grad = fs[h] * dot(a, eh, 1, 1) + dot(gw, k[:, cols(h)], 1, 0)
        qg[:, cols(h)] = grad.astype(BF16)
        kgi[h] = dot(gw, q[:, cols(h)], 0, 0)
        vgi[h] = dot(wts[h], a, 0, 0)

    late(0)
    late(1)
    rest = [(2, 3), (4, 5), (6,), (7,)]

    def fill_late():
        for h in rest.pop(0):
            late(h)
        if len(rest) == 2:
            for n in AWAY:
                gx_copy(xat(n), xat(n)).wait_recv()
            gxs[...] = gx[0] + gx[1] + gx[2] + gx[3]
            far(lambda i: gz_copy(i, z).start())
            gz[z] = gxs[pl.ds(z // (nz // HEADS), 1), :] if nz >= HEADS else gxs[pl.ds(z * (HEADS // nz), 1), :]
        if len(rest) == 0:
            bulk(gz.at[pl.ds(0, nz - 1)], gz_r.at[0]).wait_recv()
            gzs[...] = jnp.sum(gz[...], axis=0)
            each(nd, lambda i: gd_copy(dat(i), me).start())
            gd[me] = gzs[...]

    for j in range(PER):
        for p in range(2):
            for n in AWAY:
                xb_copy(0, j, p, xat(n), x).wait_send()

    scan(1, fill_late)

    for j in range(PER):
        for n in NEAR:
            i = xat(n)
            h = PER * i + j
            if n:
                for p in range(2):
                    xb_copy(1, j, p, i, i).wait_recv()
            rh = eb[1, h].astype(BF16)
            stop = te[h]
            kg[:, cols(h)] = (stop * dot(v[:, cols(h)], rh, 1, 1) + kgi[h]).astype(BF16)
            vg[:, cols(h)] = (stop * dot(k[:, cols(h)], rh, 1, 0) + vgi[h]).astype(BF16)

    bulk(gd.at[pl.ds(0, nd - 1)], gd_r.at[0]).wait_recv()
    gg[...] = jnp.sum(gd[...], axis=0)

    for n in AWAY:
        gx_copy(xat(n), x).wait_send()
    bulk(dz.at[pl.ds(0, nz - 1)], dz_s.at[0]).wait_send()
    bulk(gz.at[pl.ds(0, nz - 1)], dz_s.at[1]).wait_send()
    bulk(gd.at[pl.ds(0, nd - 1)], gd_s.at[0]).wait_send()
    for j in range(PER):
        bulk(rt.at[0, j, pl.ds(0, (nz - 1) * ch)], zs_s.at[0, j]).wait_send()
        bulk(zp.at[0, j, pl.ds(0, nz - 1)], zb_s.at[0, j]).wait_send()
    sent(1)


def write(qv, kv, vv, row, qo, ko, vo, share, held, sems):
    arrays = ((qv, qo), (kv, ko), (vv, vo))
    reads = [pltpu.make_async_copy(a, held.at[i], sems.at[0, i]) for i, (a, _) in enumerate(arrays)]
    writes = [pltpu.make_async_copy(held.at[i], b, sems.at[1, i]) for i, (_, b) in enumerate(arrays)]
    for read in reads:
        read.start()
    portion = share.shape[1]
    at = lax.rem(lax.axis_index("ctx") * portion, E)
    share[...] = pltpu.roll(row[...], lax.rem(E - at, E), 1)[:, :portion]
    for read, put in zip(reads, writes):
        read.wait()
        put.start()
    for put in writes:
        put.wait()


def body(queries, keys, values, log_decay, gain, out_grad):
    nc = lax.axis_size("ctx")
    nd = lax.axis_size("dp")
    nz = nc // NX
    ch = E // nz
    width = HEADS * E

    def vm(*shape, dtype=F32):
        return pltpu.VMEM(shape, dtype)

    dma = lambda *shape: pltpu.SemaphoreType.DMA(shape)
    flat = lambda a: a.reshape(E, width)
    hbm = pltpu.HBM
    wide = jax.ShapeDtypeStruct((E, width), BF16)
    qg, kg, vg, gg = pl.pallas_call(
        functools.partial(kernel, nz, nd),
        out_shape=(wide, wide, wide, jax.ShapeDtypeStruct((1, E), F32)),
        in_specs=[pl.BlockSpec(memory_space=m) for m in [hbm] * 6],
        out_specs=tuple([pl.BlockSpec(memory_space=pltpu.VMEM)] * 4),
        scratch_shapes=[
            *[vm(E, width, dtype=BF16)] * 4, vm(HEADS, E), vm(HEADS, E),
            vm(HEADS, E, E), vm(HEADS, E, E), vm(HEADS, E, E),
            vm(HEADS, E, E, dtype=BF16), vm(HEADS, E, E), vm(HEADS, E, E, dtype=BF16),
            vm(HEADS, E, E), vm(HEADS, E, E),
            vm(HEADS, E), vm(NX, HEADS, E), vm(PER, E), vm(nz, PER, E),
            vm(2, HEADS, E, E), vm(2, PER, NX, E, E), vm(2, PER, E, E),
            vm(2, PER, nz, ch, E), vm(2, PER, nz, ch, E), vm(2, PER, E, E),
            vm(2, PER, NX, E, E), vm(2, HEADS, E, E),
            vm(HEADS, E), vm(NX, HEADS, E), vm(HEADS, E), vm(nz, 1, E),
            vm(1, E), vm(nd, 1, E),
            dma(PER, 2, NX), dma(2, PER, 2, NX), dma(2, PER), dma(2, PER),
            dma(2, PER), dma(2, PER), dma(PER, 2, NX), dma(2, PER, 2, NX),
            dma(NX), dma(NX), dma(2), dma(1), dma(1), dma(NX), dma(1), dma(1), dma(6),
            pltpu.SemaphoreType.REGULAR, pltpu.SemaphoreType.REGULAR,
        ],
        compiler_params=pltpu.CompilerParams(
            collective_id=0, has_side_effects=True, vmem_limit_bytes=66150000
        ),
    )(
        flat(queries), flat(keys), flat(values), log_decay.reshape(HEADS, E),
        gain.reshape(HEADS, E), flat(out_grad),
    )
    portion = width // nc
    vmem = pl.BlockSpec(memory_space=pltpu.VMEM)
    away = pl.BlockSpec(memory_space=hbm)
    qg, kg, vg, share = pl.pallas_call(
        write,
        out_shape=(wide, wide, wide, jax.ShapeDtypeStruct((1, portion), F32)),
        in_specs=[pl.BlockSpec(memory_space=pl.ANY)] * 3 + [vmem],
        out_specs=(away, away, away, vmem),
        scratch_shapes=[vm(3, E, width, dtype=BF16), pltpu.SemaphoreType.DMA((2, 3))],
        compiler_params=pltpu.CompilerParams(vmem_limit_bytes=66150000),
    )(qg, kg, vg, gg)
    whole = lambda a: a.reshape(1, E, width)
    return whole(qg), whole(kg), whole(vg), share.reshape(portion)


def solution(mesh):
    in_specs = (
        P("dp", "ctx", None),
        P("dp", "ctx", None),
        P("dp", "ctx", None),
        P("dp", None, "ctx"),
        P(),
        P("dp", "ctx", None),
    )
    out_specs = (P("dp", "ctx", None), P("dp", "ctx", None), P("dp", "ctx", None), P("ctx"))
    return jax.shard_map(body, mesh=mesh, in_specs=in_specs, out_specs=out_specs, check_vma=False)
```

```python
import functools

import jax
import jax.numpy as jnp
from jax import lax
from jax.experimental import pallas as pl
from jax.experimental.pallas import tpu as pltpu
from jax.sharding import PartitionSpec as P

EPSILON = 1e-06
HEADS = 8
E = 128
NX = 4
HALF = E // 2
PER = HEADS // NX
AWAY = (2, 1, 3)
NEAR = (0, 1, 3, 2)
F32 = jnp.float32
BF16 = jnp.bfloat16
MESH = pl.DeviceIdType.MESH


def dot(a, b, ca, cb):
    return lax.dot_general(a, b, (((ca,), (cb,)), ((), ())), preferred_element_type=F32)


def kernel(nz, nd, qi, ki, vi, ldi, gaini, ogi, qo, ko, vo, gg, qg, kg, vg, q, k, v, og, ld, gain,
           fs, te, dm, wts, att, ag, kgi, vgi,
           dself, dx, drow, dz, st, xr, rt, zr, zp, zb, ex, eb,
           gt, gx, gxs, gz, gzs, gd,
           xs_s, xs_r, zs_s, zs_r, zb_s, zb_r, xb_s, xb_r,
           dx_s, dx_r, dz_s, dz_r, gd_s, gx_r, gz_r, gd_r, in_s, second_s, third_s, out_s):
    ch = E // nz
    c = lax.axis_index("ctx")
    me = lax.axis_index("dp")
    z = lax.div(c, NX)
    x = lax.rem(c, NX)

    def xat(n):
        return lax.rem(x + n, NX)

    def zat(n):
        return lax.rem(z + n, nz)

    def dat(n):
        return lax.rem(me + n, nd)

    def xdev(i):
        return {"ctx": z * NX + i}

    def zdev(i):
        return {"ctx": i * NX + x}

    def ddev(i):
        return {"dp": i}

    def rcopy(src, dst, ss, rs, dev):
        return pltpu.make_async_remote_copy(
            src_ref=src, dst_ref=dst, send_sem=ss, recv_sem=rs, device_id=dev, device_id_type=MESH
        )

    def each(count, f):
        def one(i, carry):
            f(i)
            return carry

        lax.fori_loop(1, count, one, 0)

    def far(f):
        def one(i, carry):
            f(zat(nz // 2 + ((i + 1) // 2) * (1 - 2 * (i % 2))))
            return carry

        lax.fori_loop(0, nz - 1, one, 0)

    def owners(p, f):
        def one(i, carry):
            near = (i + 1) // 2
            f(zat(nz // 2 + 2 * near * (1 - 2 * (i % 2)) + nz))
            return carry

        def other(i, carry):
            near = 2 * (i // 2) + 1
            f(zat(nz // 2 + near * (1 - 2 * (i % 2)) + nz))
            return carry

        same = (z + p + nz // 2) % 2 == 0

        @pl.when(same)
        def _():
            lax.fori_loop(0, nz // 2 - (1 if nz // 2 % 2 == 0 else 0), one, 0)

        @pl.when(jnp.logical_not(same))
        def _():
            lax.fori_loop(0, nz // 2 - (1 if nz // 2 % 2 else 0), other, 0)

    def rows(i):
        return pl.ds(pl.multiple_of(((i % 2) * (nz // 2) + i // 2) * ch, ch), ch)

    def half(p):
        return pl.ds(p * HALF, HALF)

    def bulk(ref, sem):
        return rcopy(ref, ref, sem, sem, xdev(xat(1)))

    def cols(h):
        return pl.ds(h * E if isinstance(h, int) else pl.multiple_of(h * E, E), E)

    loads = [
        pltpu.make_async_copy(a, b, in_s.at[i])
        for i, (a, b) in enumerate(((ki, k), (vi, v), (qi, q), (ogi, og), (ldi, ld), (gaini, gain)))
    ]
    for i in (4, 0, 1, 2, 3, 5):
        loads[i].start()
    barrier = pltpu.get_barrier_semaphore()
    for n in range(1, NX):
        pl.semaphore_signal(barrier, inc=1, device_id=xdev(xat(n)), device_id_type=MESH)
    for n in (1, 2, nz - 2, nz - 1):
        pl.semaphore_signal(barrier, inc=1, device_id=zdev(zat(n)), device_id_type=MESH)
    each(nd, lambda i: pl.semaphore_signal(barrier, inc=1, device_id=ddev(dat(i)), device_id_type=MESH))

    first = lax.broadcasted_iota(jnp.int32, (E, E), 0)
    second = lax.broadcasted_iota(jnp.int32, (E, E), 1)
    upper = jnp.where(first <= second, 1.0, 0.0).astype(F32)
    causal = second <= first
    loads[4].wait()
    cum = lax.dot_general(
        ld[...], upper, (((1,), (0,)), ((), ())),
        precision=lax.Precision.HIGHEST, preferred_element_type=F32,
    )
    end = cum[:, E - 1:E]
    dself[...] = jnp.exp(jnp.broadcast_to(end, (HEADS, E)))
    cum_col = cum.T
    fs_col = jnp.exp(cum).T
    te_col = jnp.exp(end - cum).T
    for h in range(HEADS):
        fs[h] = jnp.broadcast_to(fs_col[:, h:h + 1], (E, E))
        te[h] = jnp.broadcast_to(te_col[:, h:h + 1], (E, E))

    loads[0].wait()
    loads[1].wait()
    def dx_copy(i, slot):
        return rcopy(dself, dx.at[slot], dx_s.at[i], dx_r.at[slot], xdev(i))

    def dz_copy(i, slot):
        return rcopy(drow, dz.at[slot], dz_s.at[0], dz_r.at[0], zdev(i))

    def xs_copy(d, j, p, i, slot):
        return rcopy(
            st.at[d, PER * i + j, half(p)], xr.at[d, j, slot, half(p)],
            xs_s.at[j, p, i], xs_r.at[d, j, p, slot], xdev(i),
        )

    def zs_copy(d, j, i, slot):
        return rcopy(rt.at[d, j, rows(i)], zr.at[d, j, slot], zs_s.at[d, j], zs_r.at[d, j], zdev(i))

    def zb_copy(d, j, i, slot):
        return rcopy(zp.at[d, j, i], zb.at[d, j, rows(slot)], zb_s.at[d, j], zb_r.at[d, j], zdev(i))

    def xb_copy(d, j, p, i, slot):
        return rcopy(
            ex.at[d, j, i, half(p)], eb.at[d, PER * slot + j, half(p)],
            xb_s.at[j, p, i], xb_r.at[d, j, p, slot], xdev(i),
        )

    def gx_copy(i, slot):
        return rcopy(gt, gx.at[slot], dx_s.at[i], gx_r.at[slot], xdev(i))

    def gz_copy(i, slot):
        return rcopy(gxs.at[pl.ds(i // (nz // HEADS), 1)] if nz >= HEADS else gxs.at[pl.ds(i * (HEADS // nz), 1)],
                     gz.at[slot], dz_s.at[1], gz_r.at[0], zdev(i))

    def gd_copy(i, slot):
        return rcopy(gzs, gd.at[slot], gd_s.at[0], gd_r.at[0], ddev(i))

    def tell(sem, n):
        for m in (n, nz - n):
            pl.semaphore_signal(sem, inc=1, device_id=zdev(zat(m)), device_id_type=MESH)

    pl.semaphore_wait(barrier, NX - 1 + 4 + nd - 1)
    tell(second_s, 2)
    for n in AWAY:
        dx_copy(xat(n), x).start()
    dx[x] = dself[...]
    for j in range(PER):
        for n in (2, 1, 3, 0):
            h = PER * xat(n) + j
            kd = (k[:, cols(h)].astype(F32) * te[h]).astype(BF16)
            state = dot(kd, v[:, cols(h)], 0, 0)
            if n:
                st[0, h] = state
                for p in range(2):
                    xs_copy(0, j, p, xat(n), x).start()
            else:
                xr[0, j, x] = state
    pl.semaphore_wait(second_s, 2)
    if nz > 8:
        tell(third_s, 4)

    def decay(i, j):
        return dx[i, pl.ds(PER * x + j, 1), :]

    def scan(d, fill):
        steps = range(NX) if d == 0 else range(NX - 1, -1, -1)
        for j in range(PER):
            for p in range(2):
                for n in (1, 3, 2):
                    xs_copy(d, j, p, xat(n), xat(n)).wait_recv()
                total = None
                for i in steps:
                    part = xr[d, j, i, half(p)]
                    total = part if total is None else decay(i, j) * total + part
                rt[d, j, half(p)] = total
                owners(p, lambda i: zs_copy(d, j, i, z).start())
            zr[d, j, z] = rt[d, j, rows(z)]
            fill()
        for j in range(PER):
            bulk(zr.at[d, j, pl.ds(0, nz - 1)], zs_r.at[d, j]).wait_recv()
            run = jnp.zeros((ch, E), F32)
            for s in range(nz):
                i = s if d == 0 else nz - 1 - s
                zp[d, j, i] = run
                if s < nz - 1:
                    run = dz[i, j:j + 1, :] * run + zr[d, j, i]
            far(lambda i: zb_copy(d, j, i, z).start())
            zb[d, j, rows(z)] = zp[d, j, z]
            fill()
        for j in range(PER):
            bulk(zb.at[d, j, pl.ds(0, (nz - 1) * ch)], zb_r.at[d, j]).wait_recv()
            for p in range(2):
                carried = zb[d, j, half(p)]
                for s, i in enumerate(steps):
                    ex[d, j, i, half(p)] = carried
                    if s < NX - 1:
                        carried = decay(i, j) * carried + xr[d, j, i, half(p)]
                for n in AWAY:
                    xb_copy(d, j, p, xat(n), x).start()
            eb[d, PER * x + j] = ex[d, j, x]

    def sent(d):
        for j in range(PER):
            for p in range(2):
                for n in AWAY:
                    xs_copy(d, j, p, xat(n), x).wait_send()
                    xb_copy(d, j, p, xat(n), x).wait_send()
            bulk(rt.at[d, j, pl.ds(0, (nz - 1) * ch)], zs_s.at[d, j]).wait_send()
            bulk(zp.at[d, j, pl.ds(0, nz - 1)], zb_s.at[d, j]).wait_send()

    def early(h):
        own = cum_col[:, h:h + 1] - cum[h:h + 1, :]
        mask = jnp.where(causal, jnp.exp(jnp.where(causal, own, 0.0)), 0.0)
        dm[h] = mask
        w = (dot(q[:, cols(h)], k[:, cols(h)], 1, 1) * mask).astype(BF16)
        wts[h] = w
        att[h] = dot(w, v[:, cols(h)], 1, 0)

    loads[2].wait()
    early(0)
    for n in AWAY:
        dx_copy(xat(n), xat(n)).wait_recv()
    if nz > 8:
        pl.semaphore_wait(third_s, 2)
    for j in range(PER):
        drow[j:j + 1, :] = decay(0, j) * decay(1, j) * decay(2, j) * decay(3, j)
    dz[z] = drow[...]
    far(lambda i: dz_copy(i, z).start())
    early(1)
    todo = [(2, 3), (4, 5), (6,), (7,)]

    def fill_early():
        for h in todo.pop(0):
            early(h)
        if len(todo) == 2:
            bulk(dz.at[pl.ds(0, nz - 1)], dz_r.at[0]).wait_recv()

    scan(0, fill_early)

    loads[3].wait()
    loads[5].wait()
    for n in AWAY:
        dx_copy(xat(n), x).wait_send()
    for j in range(PER):
        for p in range(2):
            for n in AWAY:
                xs_copy(0, j, p, xat(n), x).wait_send()

    for j in range(PER):
        for n in NEAR:
            i = xat(n)
            h = PER * i + j
            if n:
                for p in range(2):
                    xb_copy(0, j, p, i, i).wait_recv()
            eh = eb[0, h].astype(BF16)
            qh = q[:, cols(h)]
            start = fs[h]
            attended = start * dot(qh, eh, 1, 0) + att[h]
            inverse = lax.rsqrt(jnp.mean(attended * attended, axis=-1, keepdims=True) + EPSILON)
            normed = attended * inverse
            up = og[:, cols(h)].astype(F32)
            scaled = gain[pl.ds(h, 1), :] * up
            a = (
                (scaled - normed * jnp.mean(scaled * normed, axis=-1, keepdims=True)) * inverse
            ).astype(BF16)
            ag[h] = a
            qd = (qh.astype(F32) * start).astype(BF16)
            adjoint = dot(qd, a, 0, 0)
            if n:
                st[1, h] = adjoint
                for p in range(2):
                    xs_copy(1, j, p, i, x).start()
            else:
                xr[1, j, x] = adjoint
            gt[pl.ds(h, 1), :] = jnp.sum(up * normed, axis=0, keepdims=True)
    for n in AWAY:
        gx_copy(xat(n), x).start()
    gx[x] = gt[...]

    def late(h):
        a = ag[h]
        vh = v[:, cols(h)]
        gw = (dot(a, vh, 1, 1) * dm[h]).astype(BF16)
        eh = eb[0, h].astype(BF16)
        grad = fs[h] * dot(a, eh, 1, 1) + dot(gw, k[:, cols(h)], 1, 0)
        qg[:, cols(h)] = grad.astype(BF16)
        kgi[h] = dot(gw, q[:, cols(h)], 0, 0)
        vgi[h] = dot(wts[h], a, 0, 0)

    late(0)
    late(1)
    rest = [(2, 3), (4, 5), (6,), (7,)]

    def fill_late():
        for h in rest.pop(0):
            late(h)
        if len(rest) == 2:
            for n in AWAY:
                gx_copy(xat(n), xat(n)).wait_recv()
            gxs[...] = gx[0] + gx[1] + gx[2] + gx[3]
            far(lambda i: gz_copy(i, z).start())
            gz[z] = gxs[pl.ds(z // (nz // HEADS), 1), :] if nz >= HEADS else gxs[pl.ds(z * (HEADS // nz), 1), :]
        if len(rest) == 0:
            bulk(gz.at[pl.ds(0, nz - 1)], gz_r.at[0]).wait_recv()
            gzs[...] = jnp.sum(gz[...], axis=0)
            each(nd, lambda i: gd_copy(dat(i), me).start())
            gd[me] = gzs[...]

    for j in range(PER):
        for p in range(2):
            for n in AWAY:
                xb_copy(0, j, p, xat(n), x).wait_send()

    scan(1, fill_late)
    outs = [pltpu.make_async_copy(a, b, out_s.at[i]) for i, (a, b) in enumerate(((qg, qo), (kg, ko), (vg, vo)))]
    outs[0].start()

    for j in range(PER):
        for n in NEAR:
            i = xat(n)
            h = PER * i + j
            if n:
                for p in range(2):
                    xb_copy(1, j, p, i, i).wait_recv()
            rh = eb[1, h].astype(BF16)
            stop = te[h]
            kg[:, cols(h)] = (stop * dot(v[:, cols(h)], rh, 1, 1) + kgi[h]).astype(BF16)
            vg[:, cols(h)] = (stop * dot(k[:, cols(h)], rh, 1, 0) + vgi[h]).astype(BF16)

    outs[1].start()
    outs[2].start()
    bulk(gd.at[pl.ds(0, nd - 1)], gd_r.at[0]).wait_recv()
    gg[...] = jnp.sum(gd[...], axis=0)

    for n in AWAY:
        gx_copy(xat(n), x).wait_send()
    bulk(dz.at[pl.ds(0, nz - 1)], dz_s.at[0]).wait_send()
    bulk(gz.at[pl.ds(0, nz - 1)], dz_s.at[1]).wait_send()
    bulk(gd.at[pl.ds(0, nd - 1)], gd_s.at[0]).wait_send()
    for j in range(PER):
        bulk(rt.at[0, j, pl.ds(0, (nz - 1) * ch)], zs_s.at[0, j]).wait_send()
        bulk(zp.at[0, j, pl.ds(0, nz - 1)], zb_s.at[0, j]).wait_send()
    sent(1)
    for out in outs:
        out.wait()


def write(qv, kv, vv, row, qo, ko, vo, share, held, sems):
    arrays = ((qv, qo), (kv, ko), (vv, vo))
    reads = [pltpu.make_async_copy(a, held.at[i], sems.at[0, i]) for i, (a, _) in enumerate(arrays)]
    writes = [pltpu.make_async_copy(held.at[i], b, sems.at[1, i]) for i, (_, b) in enumerate(arrays)]
    for read in reads:
        read.start()
    portion = share.shape[1]
    at = lax.rem(lax.axis_index("ctx") * portion, E)
    share[...] = pltpu.roll(row[...], lax.rem(E - at, E), 1)[:, :portion]
    for read, put in zip(reads, writes):
        read.wait()
        put.start()
    for put in writes:
        put.wait()


def body(queries, keys, values, log_decay, gain, out_grad):
    nc = lax.axis_size("ctx")
    nd = lax.axis_size("dp")
    nz = nc // NX
    ch = E // nz
    width = HEADS * E

    def vm(*shape, dtype=F32):
        return pltpu.VMEM(shape, dtype)

    dma = lambda *shape: pltpu.SemaphoreType.DMA(shape)
    flat = lambda a: a.reshape(E, width)
    hbm = pltpu.HBM
    wide = jax.ShapeDtypeStruct((E, width), BF16)
    qg, kg, vg, gg = pl.pallas_call(
        functools.partial(kernel, nz, nd),
        out_shape=(wide, wide, wide, jax.ShapeDtypeStruct((1, E), F32)),
        in_specs=[pl.BlockSpec(memory_space=m) for m in [hbm] * 6],
        out_specs=tuple(pl.BlockSpec(memory_space=m) for m in (hbm, hbm, hbm, pltpu.VMEM)),
        scratch_shapes=[
            *[vm(E, width, dtype=BF16)] * 7, vm(HEADS, E), vm(HEADS, E),
            vm(HEADS, E, E), vm(HEADS, E, E), vm(HEADS, E, E),
            vm(HEADS, E, E, dtype=BF16), vm(HEADS, E, E), vm(HEADS, E, E, dtype=BF16),
            vm(HEADS, E, E), vm(HEADS, E, E),
            vm(HEADS, E), vm(NX, HEADS, E), vm(PER, E), vm(nz, PER, E),
            vm(2, HEADS, E, E), vm(2, PER, NX, E, E), vm(2, PER, E, E),
            vm(2, PER, nz, ch, E), vm(2, PER, nz, ch, E), vm(2, PER, E, E),
            vm(2, PER, NX, E, E), vm(2, HEADS, E, E),
            vm(HEADS, E), vm(NX, HEADS, E), vm(HEADS, E), vm(nz, 1, E),
            vm(1, E), vm(nd, 1, E),
            dma(PER, 2, NX), dma(2, PER, 2, NX), dma(2, PER), dma(2, PER),
            dma(2, PER), dma(2, PER), dma(PER, 2, NX), dma(2, PER, 2, NX),
            dma(NX), dma(NX), dma(2), dma(1), dma(1), dma(NX), dma(1), dma(1), dma(6),
            pltpu.SemaphoreType.REGULAR, pltpu.SemaphoreType.REGULAR, dma(3),
        ],
        compiler_params=pltpu.CompilerParams(
            collective_id=0, has_side_effects=True, vmem_limit_bytes=66150000
        ),
    )(
        flat(queries), flat(keys), flat(values), log_decay.reshape(HEADS, E),
        gain.reshape(HEADS, E), flat(out_grad),
    )
    portion = width // nc
    vmem = pl.BlockSpec(memory_space=pltpu.VMEM)
    away = pl.BlockSpec(memory_space=hbm)
    qg, kg, vg, share = pl.pallas_call(
        write,
        out_shape=(wide, wide, wide, jax.ShapeDtypeStruct((1, portion), F32)),
        in_specs=[pl.BlockSpec(memory_space=pl.ANY)] * 3 + [vmem],
        out_specs=(away, away, away, vmem),
        scratch_shapes=[vm(3, E, width, dtype=BF16), pltpu.SemaphoreType.DMA((2, 3))],
        compiler_params=pltpu.CompilerParams(vmem_limit_bytes=66150000),
    )(qg, kg, vg, gg)
    whole = lambda a: a.reshape(1, E, width)
    return whole(qg), whole(kg), whole(vg), share.reshape(portion)


def solution(mesh):
    in_specs = (
        P("dp", "ctx", None),
        P("dp", "ctx", None),
        P("dp", "ctx", None),
        P("dp", None, "ctx"),
        P(),
        P("dp", "ctx", None),
    )
    out_specs = (P("dp", "ctx", None), P("dp", "ctx", None), P("dp", "ctx", None), P("ctx"))
    return jax.shard_map(body, mesh=mesh, in_specs=in_specs, out_specs=out_specs, check_vma=False)
```
